32 devices in a mesh: runs: 2 (over y), panel: 4 (over z), sub: 2 (over x), case: 2 (over core).
Axes of the slice: x: 2, y: 2, z: 4, core: 2. Of those that a mesh axis runs over, the one named last changes fastest.
Arguments:
- case_index: int32 [8], P(('runs', 'case')), parts along dimension 0, may hold values from 0 to 7
- case_library: bfloat16 [8, 64, 256], replicated, may hold values from -6 to 6
- panel_zone: int32 [2048], P('panel'), may hold values from 0 to 63
- panel_gain: float32 [8, 2048], P(('runs', 'case'), 'panel'), parts along dimension 0, may hold values from 0.3 to 3
- fluctuation: bfloat16 [8, 256, 2048], P(('runs', 'case'), None, 'panel'), parts along dimension 0, may hold values from -4 to 4
- mode_shapes: bfloat16 [2048, 4096], P('panel', 'sub'), may hold values from -0.1875 to 0.1875
- mode_frequency: float32 [4096], P('sub'), may hold values from 0.03 to 1.2
- mode_damping: float32 [8192], P(('runs', 'sub')), parts along dimension 0, may hold values from 0.01 to 0.2
- span_id: int32 [8, 256], P(('runs', 'case')), parts along dimension 0, may hold values from 0 to 3, never falling along the last dimension, each value on 1 to 128 neighbouring positions
- load_matrix: bfloat16 [3072, 4096], P('panel', 'sub'), may hold values from -0.125 to 0.125
Outputs:
- responses: bfloat16 [8, 256, 2, 2048], P(('runs', 'case'), None, 'sub', 'panel'), parts along dimension 0
- element_loads: bfloat16 [8, 256, 3072], P(('runs', 'case'), None, ('panel', 'sub')), parts along dimension 0
The draws below stay inside these ranges and needn't reach their ends.
There are 2 independent parts, one for each index of `runs`. The reference program is written for one: setup_inputs(seed, part) draws one part's arguments, and reference() takes and returns one part's arrays. A program takes and returns all parts, laid end to end along the dimension named above; an argument that names none is the same for every part. Nothing has to cross between parts.
Inputs may be any that keep to these rules, and one draw needn't show every extreme that they name: `span_id`: each case's row never falls; each block value covers 1 to 128 steps, and some block exactly 128.
All inputs are finite; a program needn't handle non-finite values.
Results may differ from the reference program's by a relative error of at most 0.0057.
Values may be sent and summed in bfloat16 or wider, within the bound.
No kernel may reach another device: no remote copies, remote signals or barrier semaphores. Data moves between devices by JAX's collectives and lax.ppermute only.
A program may use at most 64 MiB of HBM per device.

```python
import math
import jax
import jax.numpy as jnp
import numpy as np
from jax import lax

MODES = 4096
STEPS = 256
ZONES = 64
LIB = 8
SEGS = 4
CASES = 4
PANELS = 2048
LROWS = 3072
N_SUB = 2


def touch_ends(values, rng, smallest, top_value):
    dims = values.shape
    index_at = [jax.random.randint(jax.random.fold_in(rng, axis), (), 0, dims[axis]) for axis in range(len(dims))]
    values = values.at[tuple(index_at)].set(smallest)
    longest = dims.index(max(dims))
    index_at[longest] = (index_at[longest] + 1) % dims[longest]
    return values.at[tuple(index_at)].set(top_value)


def with_spikes(entries, stream_key, source, target, parts, factor):
    def block_of(position):
        return (jnp.arange(entries.shape[position]) // (entries.shape[position] // parts)).reshape((-1,) + (1,) * (entries.ndim - 1 - position))

    one_side = jax.random.permutation(stream_key, parts)[block_of(target)]
    other_side = (block_of(target) + parts // 2) % parts
    return jnp.where((block_of(source) == one_side) | (block_of(source) == other_side), factor * entries, entries)


def shard_levels(key, dims, split, smallest, high):
    def one(axis_at, blocks):
        steps = jax.random.uniform(jax.random.fold_in(jax.random.fold_in(key, 6), axis_at), (blocks,), jnp.float32, smallest / len(split), high / len(split))
        return jnp.repeat(jnp.exp(steps), dims[axis_at] // blocks).reshape((-1,) + (1,) * (len(dims) - axis_at - 1))

    factor_of = one(*split[0])
    for cut in split[1:]:
        factor_of = factor_of * one(*cut)
    return factor_of


def profile(number_of, total, reach, lean):
    loads = [(1 << 20) // math.isqrt(rank ** lean) + 1 for rank in range(2, number_of + 1)]
    surplus, holding = total - reach - (number_of - 1), [1] * (number_of - 1)
    while surplus > 0:
        candidates = [i for i in range(number_of - 1) if holding[i] < reach]
        whole, left = sum([loads[i] for i in candidates]), surplus
        for i in candidates:
            extra = min(reach - holding[i], max(1, left * loads[i] // whole), surplus)
            holding[i] = holding[i] + extra
            surplus = surplus - extra
    return np.array([reach] + holding)


def ragged_sizes(rng, amount, total, bound, slope):
    if amount == 2:
        one = jax.random.randint(rng, (), max(1, total - bound), min(bound, total - 1) + 1)
        return jnp.stack([one, total - one])
    lengths = jnp.asarray(profile(amount, total, bound, slope), jnp.int32)
    couples = (amount - 1) // 2
    donor, sink = lengths[1:1 + 2 * couples:2], lengths[2:2 + 2 * couples:2]
    slack = jnp.minimum(donor - 1, bound - sink)
    shifted = jax.random.randint(jax.random.fold_in(rng, 1), (couples,), 0, 1 << 20) % (slack + 1)
    lengths = lengths.at[1:1 + 2 * couples:2].set(donor - shifted).at[2:2 + 2 * couples:2].set(sink + shifted)
    return lengths[jax.random.permutation(jax.random.fold_in(rng, 2), amount)]


def normal_values(stream_key, shape, scale, bound, shards=(), kind=jnp.bfloat16):
    drawn = jax.random.normal(stream_key, shape, jnp.float32) * scale
    if len(shards) > 0:
        drawn = shard_levels(stream_key, shape, shards, -0.22, 0.18) * drawn
    return jnp.clip(drawn, min=-bound, max=bound).astype(kind)


def bell_draw_with(stream_key, shape, scale, bound, split, heavy, kind=jnp.bfloat16):
    result = scale * jax.random.normal(stream_key, shape, jnp.float32)
    if split:
        result = result * shard_levels(stream_key, shape, split, -0.22, 0.18)
    return jnp.clip(with_spikes(result, jax.random.fold_in(stream_key, 3), *heavy), -bound, bound).astype(kind)


def setup_inputs(seed: int = 0, part: int = 0) -> dict:
    key_list = jax.random.split(jax.random.key(seed), 11)
    own_keys = jax.random.split(jax.random.fold_in(key_list[10], part), 11)
    case_index = touch_ends(jax.random.randint(own_keys[0], (CASES,), 0, LIB), jax.random.fold_in(own_keys[0], 1), 0, LIB - 1).astype(jnp.int32)
    case_library = normal_values(key_list[1], (LIB, ZONES, STEPS), 1.0, 6.0)
    panel_zone = touch_ends(jax.random.randint(key_list[2], (PANELS,), 0, ZONES), jax.random.fold_in(key_list[2], 1), 0, ZONES - 1).astype(jnp.int32)
    panel_gain = jnp.clip(jnp.exp(math.log(3.0) - 2.3025851 * jax.random.uniform(own_keys[3], (CASES, PANELS), jnp.float32) ** shard_levels(own_keys[3], (CASES, PANELS), ((0, 2), (1, 4)), -0.2, 0.2)), 0.3, 3.0)
    fluctuation = normal_values(own_keys[4], (CASES, STEPS, PANELS), 0.5, 4.0, ((0, 2), (2, 4)))
    mode_shapes = bell_draw_with(key_list[5], (PANELS, MODES), PANELS ** -0.5, 0.1875, ((0, 4), (1, 2)), (0, 1, 4, 2.0))
    mode_frequency = jnp.clip(jnp.exp(math.log(1.2) - 3.6888795 * jax.random.uniform(key_list[6], (MODES,), jnp.float32) ** shard_levels(key_list[6], (MODES,), ((0, 2),), -0.2, 0.2)), 0.03, 1.2)
    mode_damping = jnp.clip(jnp.exp(math.log(0.2) - 2.9957323 * jax.random.uniform(own_keys[7], (MODES,), jnp.float32) ** shard_levels(own_keys[7], (MODES,), ((0, 2),), -0.2, 0.2)), 0.01, 0.2)
    span_id = jax.vmap(lambda own: jnp.searchsorted(jnp.cumsum(ragged_sizes(own, SEGS, STEPS, STEPS // 2, 0)), jnp.arange(STEPS), side="right"))(jax.random.split(own_keys[8], CASES)).reshape((CASES, STEPS)).astype(jnp.int32)
    load_matrix = bell_draw_with(key_list[9], (LROWS, MODES), MODES ** -0.5, 0.125, ((0, 4), (1, 2)), (1, 0, 4, 2.0))
    return {"case_index": case_index, "case_library": case_library, "panel_zone": panel_zone, "panel_gain": panel_gain, "fluctuation": fluctuation, "mode_shapes": mode_shapes, "mode_frequency": mode_frequency, "mode_damping": mode_damping, "span_id": span_id, "load_matrix": load_matrix}


def modal_kernel(frequency, damping, length):
    decay_rate = frequency * damping
    lagged = jnp.arange(length)[:, None] - jnp.arange(length)[None, :]
    causal = lagged >= 0
    delay_steps = jnp.maximum(lagged, 0).astype(jnp.float32)
    amplitude = jnp.sqrt(2.0 * decay_rate + 2.0 / length)
    values = amplitude[:, None, None] * jnp.exp(-decay_rate[:, None, None] * delay_steps) * jnp.cos(frequency[:, None, None] * delay_steps)
    return jnp.where(causal[None], values, 0.0)

def span_masks(span_id):
    return span_id[:, :, None] == span_id[:, None, :]

def respond(forces, frequency, damping, same_span):
    toeplitz = modal_kernel(frequency, damping, forces.shape[2])
    outputs = []
    for member in range(forces.shape[1]):
        masked = jnp.where(same_span[member][None], toeplitz, 0.0)
        outputs.append(jnp.einsum('mts,ms->mt', masked, forces[:, member, :], precision=lax.Precision.HIGHEST))
    return jnp.stack(outputs, axis=1)

def reference(case_index, case_library, panel_zone, panel_gain, fluctuation, mode_shapes, mode_frequency, mode_damping, span_id, load_matrix):
    zone_load = case_library[case_index]
    spread = jnp.transpose(zone_load[:, panel_zone, :], (0, 2, 1)).astype(jnp.float32)
    pressure = (panel_gain[:, None, :] * spread + fluctuation.astype(jnp.float32)).astype(jnp.bfloat16)
    members = pressure.shape[0]
    length = pressure.shape[1]
    forces = jnp.dot(pressure.reshape(members * length, -1), mode_shapes, preferred_element_type=jnp.float32)
    block_modes = min(MODES, 128)
    grouped = forces.reshape(members, length, MODES // block_modes, block_modes).transpose(2, 3, 0, 1)
    same_span = span_masks(span_id)

    def one_block(packed):
        block_forces, frequency, damping = packed
        return respond(block_forces, frequency, damping, same_span)
    answers = lax.map(one_block, (grouped, mode_frequency.reshape(-1, block_modes), mode_damping.reshape(-1, block_modes)))
    modal = answers.transpose(2, 3, 0, 1).reshape(members, length, MODES).astype(jnp.bfloat16)
    element_sums = jnp.dot(modal.reshape(members * length, MODES), load_matrix.T, preferred_element_type=jnp.float32)
    return (modal.reshape(members, length, N_SUB, MODES // N_SUB), element_sums.astype(jnp.bfloat16).reshape(members, length, -1))
```

```python
import functools

import jax
import jax.numpy as jnp
from jax import lax
from jax.experimental import pallas as pl
from jax.experimental.pallas import tpu as pltpu
from jax.sharding import PartitionSpec as P

BLOCKS = 8
LANES = 128


def pressure_of(library_ref, zone_ref, gain_ref, fluctuation_ref, member):
    zones = library_ref.shape[1]
    panels = zone_ref.shape[1]
    onehot = (
        lax.broadcasted_iota(jnp.int32, (zones, panels), 0) == zone_ref[...]
    ).astype(jnp.bfloat16)
    spread = lax.dot_general(
        library_ref[0], onehot, (((0,), (0,)), ((), ())), preferred_element_type=jnp.float32
    )
    gain = gain_ref[member : member + 1, :]
    return (gain * spread + fluctuation_ref[0].astype(jnp.float32)).astype(jnp.bfloat16)


def forces_kernel(
    member, index_ref, order_ref, library_ref, zone_ref, gain_ref, fluctuation_ref, shapes_ref, *out_refs
):
    pressure = pressure_of(library_ref, zone_ref, gain_ref, fluctuation_ref, member)
    width = out_refs[0].shape[1]
    for slot, out_ref in enumerate(out_refs):
        if len(out_refs) == 1:
            columns = shapes_ref[...]
        else:
            start = pl.multiple_of(order_ref[slot] * width, LANES)
            columns = shapes_ref[:, pl.ds(start, width)]
        out_ref[...] = jnp.dot(
            pressure, columns, preferred_element_type=jnp.float32
        ).astype(out_ref.dtype)


def forces_call(member, case_index, order, library, zone, gain, fluctuation, shapes, pieces, kind):
    _, zones, length = library.shape
    panels, modes = shapes.shape
    width = modes // pieces
    whole = lambda i, index, order: (0, 0)
    grid_spec = pltpu.PrefetchScalarGridSpec(
        num_scalar_prefetch=2,
        grid=(1,),
        in_specs=[
            pl.BlockSpec((1, zones, length), lambda i, index, order: (index[member], 0, 0)),
            pl.BlockSpec((1, panels), whole),
            pl.BlockSpec(gain.shape, whole),
            pl.BlockSpec((1, length, panels), lambda i, index, order: (member, 0, 0)),
            pl.BlockSpec((panels, modes), whole),
        ],
        out_specs=[pl.BlockSpec((length, width), whole)] * pieces,
    )
    flops = 2 * length * panels * (modes + zones)
    return pl.pallas_call(
        functools.partial(forces_kernel, member),
        grid_spec=grid_spec,
        out_shape=[jax.ShapeDtypeStruct((length, width), kind)] * pieces,
        cost_estimate=pl.CostEstimate(
            flops=flops, transcendentals=0, bytes_accessed=2 * (panels * modes + length * (modes + panels))
        ),
        name=f"forces{member}",
    )(case_index, order, library, zone[None, :], gain, fluctuation, shapes)


def modal_kernel(count, *refs):
    part_refs, keep_ref, coef_ref, out_ref, total_ref = (
        refs[:count], refs[count], refs[count + 1], refs[count + 2], refs[count + 3],
    )
    length, modes = out_ref.shape
    steps = length // BLOCKS
    groups = modes // LANES
    first_row = lax.broadcasted_iota(jnp.int32, (BLOCKS, LANES), 0) == 0

    def rows(step):
        return pl.ds(step, BLOCKS, stride=steps)

    decay_re, decay_im, amplitude = [], [], []
    for g in range(groups):
        at = pl.ds(g * LANES, LANES)
        total = part_refs[0][:, at].astype(jnp.float32)
        for part_ref in part_refs[1:]:
            total = total + part_ref[:, at].astype(jnp.float32)
        total_ref[g] = total
        decay_re.append(jnp.broadcast_to(coef_ref[0:1, at], (BLOCKS, LANES)))
        decay_im.append(jnp.broadcast_to(coef_ref[1:2, at], (BLOCKS, LANES)))
        amplitude.append(jnp.broadcast_to(coef_ref[2:3, at], (BLOCKS, LANES)))

    def advance(step, re, im):
        keep = keep_ref[rows(step), :]
        for g in range(groups):
            a, b = decay_re[g], decay_im[g]
            force = total_ref[g, rows(step), :]
            held_re, held_im = keep * re[g], keep * im[g]
            re[g] = (a * held_re - b * held_im) + force
            im[g] = b * held_re + a * held_im
        return keep

    zero = jnp.zeros((BLOCKS, LANES), jnp.float32)
    re, im = [zero] * groups, [zero] * groups
    through = jnp.ones((BLOCKS, LANES), jnp.float32)
    for step in range(steps):
        through = through * advance(step, re, im)

    start_re, start_im = [], []
    for g in range(groups):
        power_re, power_im = jnp.ones_like(zero), zero
        square_re, square_im = decay_re[g], decay_im[g]
        left = steps
        while left:
            if left % 2:
                power_re, power_im = (
                    power_re * square_re - power_im * square_im,
                    power_re * square_im + power_im * square_re,
                )
            square_re, square_im = (
                square_re * square_re - square_im * square_im,
                2.0 * square_re * square_im,
            )
            left //= 2
        power_re, power_im = through * power_re, through * power_im
        end_re, end_im = re[g], im[g]
        carried_re, carried_im = zero, zero
        for _ in range(BLOCKS - 1):
            full_re = end_re + power_re * carried_re - power_im * carried_im
            full_im = end_im + power_re * carried_im + power_im * carried_re
            carried_re = jnp.where(first_row, 0.0, pltpu.roll(full_re, 1, 0))
            carried_im = jnp.where(first_row, 0.0, pltpu.roll(full_im, 1, 0))
        start_re.append(carried_re)
        start_im.append(carried_im)

    re, im = start_re, start_im
    for step in range(steps):
        advance(step, re, im)
        for g in range(groups):
            total_ref[g, rows(step), :] = amplitude[g] * re[g]
    for g in range(groups):
        out_ref[:, pl.ds(g * LANES, LANES)] = total_ref[g].astype(out_ref.dtype)


def modal_call(parts, keep, coefficients, name):
    length, modes = parts[0].shape
    spare = -modes % LANES
    if spare:
        parts = [jnp.pad(part, ((0, 0), (0, spare))) for part in parts]
        coefficients = jnp.pad(coefficients, ((0, 0), (0, spare)))
    width = modes + spare
    modal = pl.pallas_call(
        functools.partial(modal_kernel, len(parts)),
        out_shape=jax.ShapeDtypeStruct((length, width), jnp.bfloat16),
        scratch_shapes=[pltpu.VMEM((width // LANES, length, LANES), jnp.float32)],
        cost_estimate=pl.CostEstimate(
            flops=40 * length * width, transcendentals=0, bytes_accessed=8 * length * width
        ),
        name=name,
    )(*parts, keep, coefficients)
    return modal[:, :modes] if spare else modal


def loads_kernel(where_ref, matrix_ref, own_ref, near_ref, *refs):
    middle_refs, send_ref, stay_ref = refs[:-2], refs[-2], refs[-1]
    width = own_ref.shape[1]
    rows = send_ref.shape[1]
    shards = [own_ref[...], near_ref[...]]
    for a_ref, b_ref in zip(middle_refs[0::2], middle_refs[1::2]):
        shards.append(a_ref[...] + b_ref[...])
    for slot, out_ref in ((0, send_ref), (1, stay_ref)):
        first = pl.multiple_of(where_ref[4 + slot] * rows, 16)
        total = None
        for position, shard in enumerate(shards):
            start = pl.multiple_of(where_ref[position] * width, LANES)
            block = matrix_ref[pl.ds(first, rows), pl.ds(start, width)]
            product = lax.dot_general(
                shard, block, (((1,), (1,)), ((), ())), preferred_element_type=jnp.float32
            )
            total = product if total is None else total + product
        out_ref[...] = total.astype(out_ref.dtype)


def loads_call(where, matrix, shards, name):
    rows, modes = matrix.shape
    length = shards[0].shape[0]
    return pl.pallas_call(
        loads_kernel,
        in_specs=[pl.BlockSpec(memory_space=pltpu.SMEM)]
        + [pl.BlockSpec(memory_space=pltpu.VMEM)] * (1 + len(shards)),
        out_shape=[
            jax.ShapeDtypeStruct((length, rows // 2), jnp.bfloat16),
            jax.ShapeDtypeStruct((length, rows // 2), jnp.float32),
        ],
        cost_estimate=pl.CostEstimate(
            flops=2 * length * rows * modes, transcendentals=0, bytes_accessed=2 * rows * modes
        ),
        name=name,
    )(where, matrix, *shards)


def recurrence(frequency, damping, span_id):
    length = span_id.shape[1]
    decay_rate = frequency * damping
    magnitude = jnp.exp(-decay_rate)
    coefficients = jnp.stack(
        [
            magnitude * jnp.cos(frequency),
            magnitude * jnp.sin(frequency),
            jnp.sqrt(2.0 * decay_rate + 2.0 / length),
        ]
    )
    same = jnp.pad(span_id[:, 1:] == span_id[:, :-1], ((0, 0), (1, 0)))
    keep = jnp.broadcast_to(same.astype(jnp.float32)[:, :, None], span_id.shape + (LANES,))
    return coefficients, keep


def line_body(
    case_index, library, zone, gain, fluctuation, shapes, frequency, damping, span_id, matrix
):
    members, length, _ = fluctuation.shape
    own = shapes.shape[1] // 4
    z = lax.axis_index("panel")
    x = lax.axis_index("sub")
    left = z < 2
    end = (z == 0) | (z == 3)
    pick = lambda table: jnp.asarray(table, jnp.int32)[:, z]
    order = pick([[3, 0, 3, 0], [2, 3, 0, 1], [1, 2, 1, 2], [0, 1, 2, 3]])
    shard_at = pick([[0, 1, 2, 3], [1, 0, 3, 2], [2, 2, 1, 1], [3, 3, 0, 0]])
    where = jnp.concatenate([shard_at, jnp.stack([1 - x, x])]).astype(jnp.int32)
    inner = [(0, 1), (1, 0), (2, 3), (3, 2)]
    inward = [(0, 1), (3, 2)]
    outward = [(1, 0), (2, 3)]
    middle = [(1, 2), (2, 1)]
    move = lambda value, pairs: lax.ppermute(value, "panel", pairs)

    coefficients, keep = recurrence(
        lax.dynamic_slice_in_dim(frequency, z * own, own, 0),
        lax.dynamic_slice_in_dim(damping, z * own, own, 0),
        span_id,
    )

    pieces = [
        forces_call(m, case_index, order, library, zone, gain, fluctuation, shapes, 4, jnp.bfloat16)
        for m in range(members)
    ]
    out0, out1, out2, out3 = [jnp.concatenate(p, axis=0) for p in zip(*pieces)]
    first = move(out0, inner)
    second = move(out1, inward)
    far = move(out1 + first, middle)
    third = move(jnp.where(end, out2, far), inner)
    near = move(out2 + second, middle)
    other = jnp.where(end, first, near)

    at = lambda value, m: value[m * length : (m + 1) * length]
    modal = [
        modal_call([at(out3, m), at(third, m), at(other, m)], keep[m], coefficients, f"modal{m}")
        for m in range(members)
    ]
    responses = jnp.stack(modal)[:, :, None, :]
    flat = jnp.concatenate(modal, axis=0)
    pair = move(flat, inner)
    across = move(flat, middle)
    across_end = move(pair, middle)
    from_mid = move(across, outward)
    from_end = move(across_end, outward)
    send, stay = loads_call(where, matrix, [flat, pair, across, from_mid, across_end, from_end], "loads")
    got = lax.ppermute(send, "sub", [(0, 1), (1, 0)])
    element = (stay + got.astype(jnp.float32)).astype(jnp.bfloat16)
    return responses, element.reshape(members, length, -1)


def general_body(
    case_index, library, zone, gain, fluctuation, shapes, frequency, damping, span_id, matrix
):
    members, length, _ = fluctuation.shape
    own = shapes.shape[1] // lax.axis_size("panel")
    order = jnp.zeros((1,), jnp.int32)
    z = lax.axis_index("panel")
    coefficients, keep = recurrence(
        lax.dynamic_slice_in_dim(frequency, z * own, own, 0),
        lax.dynamic_slice_in_dim(damping, z * own, own, 0),
        span_id,
    )
    partial = jnp.concatenate(
        [
            forces_call(m, case_index, order, library, zone, gain, fluctuation, shapes, 1, jnp.float32)[0]
            for m in range(members)
        ],
        axis=0,
    )
    forces = jnp.transpose(
        lax.psum_scatter(jnp.transpose(partial), "panel", scatter_dimension=0, tiled=True)
    )
    modal = [
        modal_call([forces[m * length : (m + 1) * length]], keep[m], coefficients, f"modal{m}")
        for m in range(members)
    ]
    responses = jnp.stack(modal)[:, :, None, :]
    flat = jnp.transpose(jnp.concatenate(modal, axis=0))
    partial_loads = jnp.dot(
        matrix,
        lax.all_gather(flat, "panel", axis=0, tiled=True),
        preferred_element_type=jnp.float32,
    )
    sums = lax.psum_scatter(partial_loads, "sub", scatter_dimension=0, tiled=True)
    element = jnp.transpose(sums.astype(jnp.bfloat16)).reshape(members, length, -1)
    return responses, element


def solution(mesh):
    in_specs = (
        P(("runs", "case")),
        P(),
        P("panel"),
        P(("runs", "case"), "panel"),
        P(("runs", "case"), None, "panel"),
        P("panel", "sub"),
        P("sub"),
        P(("runs", "sub")),
        P(("runs", "case"), None),
        P("panel", "sub"),
    )
    out_specs = (
        P(("runs", "case"), None, "sub", "panel"),
        P(("runs", "case"), None, ("panel", "sub")),
    )
    line = mesh.shape["panel"] == 4 and mesh.shape["sub"] == 2
    return jax.shard_map(
        line_body if line else general_body,
        mesh=mesh,
        in_specs=in_specs,
        out_specs=out_specs,
        check_vma=False,
    )
```

```python
import functools

import jax
import jax.numpy as jnp
from jax import lax
from jax.experimental import pallas as pl
from jax.experimental.pallas import tpu as pltpu
from jax.sharding import PartitionSpec as P

BLOCKS = 8
LANES = 128
GRANT = 16 << 20
SMALL_GRANT = 4 << 20


def line_place():
    z = lax.axis_index("panel")
    return z, (z == 0) | (z == 3)


def line_order(z):
    far = jnp.where(z < 2, 3, 0)
    inner = (z == 1) | (z == 2)
    return (
        jnp.where(z % 2 == 0, 3, 0),
        jnp.where(inner, far, jnp.where(z == 0, 2, 1)),
        jnp.where(z % 2 == 0, 1, 2),
        z,
    )


def pressure_of(library_ref, zone_ref, gain_ref, fluctuation_ref, member):
    zones = library_ref.shape[1]
    panels = zone_ref.shape[1]
    onehot = (
        lax.broadcasted_iota(jnp.int32, (zones, panels), 0) == zone_ref[...]
    ).astype(jnp.bfloat16)
    spread = lax.dot_general(
        library_ref[0], onehot, (((0,), (0,)), ((), ())), preferred_element_type=jnp.float32
    )
    gain = gain_ref[member : member + 1, :]
    return (gain * spread + fluctuation_ref[0].astype(jnp.float32)).astype(jnp.bfloat16)


def forces_kernel(
    member, index_ref, library_ref, zone_ref, gain_ref, fluctuation_ref, shapes_ref, *out_refs
):
    pressure = pressure_of(library_ref, zone_ref, gain_ref, fluctuation_ref, member)
    width = out_refs[0].shape[1]
    order = line_order(line_place()[0]) if len(out_refs) > 1 else None
    for slot, out_ref in enumerate(out_refs):
        if order is None:
            columns = shapes_ref[...]
        else:
            columns = shapes_ref[:, pl.ds(pl.multiple_of(order[slot] * width, LANES), width)]
        out_ref[...] = jnp.dot(
            pressure, columns, preferred_element_type=jnp.float32
        ).astype(out_ref.dtype)


def forces_call(member, case_index, library, zone, gain, fluctuation, shapes, kinds):
    _, zones, length = library.shape
    panels, modes = shapes.shape
    pieces = len(kinds)
    width = modes // pieces
    once = pl.Buffered(1)
    whole = lambda i, index: (0, 0)
    grid_spec = pltpu.PrefetchScalarGridSpec(
        num_scalar_prefetch=1,
        grid=(1,),
        in_specs=[
            pl.BlockSpec((1, zones, length), lambda i, index: (index[member], 0, 0), pipeline_mode=once),
            pl.BlockSpec((1, panels), whole, pipeline_mode=once),
            pl.BlockSpec(gain.shape, whole, pipeline_mode=once),
            pl.BlockSpec((1, length, panels), lambda i, index: (member, 0, 0), pipeline_mode=once),
            pl.BlockSpec((panels, modes), whole, pipeline_mode=once),
        ],
        out_specs=[pl.BlockSpec((length, width), whole, pipeline_mode=once)] * pieces,
    )
    flops = 2 * length * panels * (modes + zones)
    return pl.pallas_call(
        functools.partial(forces_kernel, member),
        grid_spec=grid_spec,
        out_shape=[jax.ShapeDtypeStruct((length, width), kind) for kind in kinds],
        cost_estimate=pl.CostEstimate(
            flops=flops, transcendentals=0, bytes_accessed=2 * (panels * modes + length * (modes + panels))
        ),
        compiler_params=pltpu.CompilerParams(vmem_limit_bytes=GRANT),
        name=f"forces{member}",
    )(case_index, library, zone[None, :], gain, fluctuation, shapes)


def add_kernel(a_ref, b_ref, out_ref):
    out_ref[...] = (a_ref[...].astype(jnp.float32) + b_ref[...].astype(jnp.float32)).astype(
        out_ref.dtype
    )


def choose_kernel(end_ref, inner_ref, out_ref):
    _, end = line_place()

    @pl.when(end)
    def _():
        out_ref[...] = end_ref[...]

    @pl.when(jnp.logical_not(end))
    def _():
        out_ref[...] = inner_ref[...]


def small_call(kernel, a, b, name):
    return pl.pallas_call(
        kernel,
        out_shape=jax.ShapeDtypeStruct(a.shape, a.dtype),
        cost_estimate=pl.CostEstimate(flops=a.size, transcendentals=0, bytes_accessed=6 * a.size),
        compiler_params=pltpu.CompilerParams(vmem_limit_bytes=SMALL_GRANT),
        name=name,
    )(a, b)


def modal_kernel(count, *refs):
    part_refs, keep_ref, coef_ref, out_ref, total_ref = (
        refs[:count], refs[count], refs[count + 1], refs[count + 2], refs[count + 3],
    )
    length, modes = out_ref.shape
    steps = length // BLOCKS
    groups = modes // LANES
    first_row = lax.broadcasted_iota(jnp.int32, (BLOCKS, LANES), 0) == 0

    def rows(step):
        return pl.ds(step, BLOCKS, stride=steps)

    decay_re, decay_im, amplitude = [], [], []
    for g in range(groups):
        at = pl.ds(g * LANES, LANES)
        total = part_refs[0][:, at]
        if count > 1:
            total = total + part_refs[1][:, at].astype(jnp.float32)
            _, end = line_place()
            total = total + jnp.where(end, part_refs[2][:, at], part_refs[3][:, at]).astype(
                jnp.float32
            )
        total_ref[g] = total
        decay_re.append(jnp.broadcast_to(coef_ref[0:1, at], (BLOCKS, LANES)))
        decay_im.append(jnp.broadcast_to(coef_ref[1:2, at], (BLOCKS, LANES)))
        amplitude.append(jnp.broadcast_to(coef_ref[2:3, at], (BLOCKS, LANES)))

    def advance(step, re, im):
        keep = keep_ref[rows(step), :]
        for g in range(groups):
            a, b = decay_re[g], decay_im[g]
            force = total_ref[g, rows(step), :]
            held_re, held_im = keep * re[g], keep * im[g]
            re[g] = (a * held_re - b * held_im) + force
            im[g] = b * held_re + a * held_im
        return keep

    zero = jnp.zeros((BLOCKS, LANES), jnp.float32)
    re, im = [zero] * groups, [zero] * groups
    through = jnp.ones((BLOCKS, LANES), jnp.float32)
    for step in range(steps):
        through = through * advance(step, re, im)

    start_re, start_im = [], []
    for g in range(groups):
        power_re, power_im = jnp.ones_like(zero), zero
        square_re, square_im = decay_re[g], decay_im[g]
        left = steps
        while left:
            if left % 2:
                power_re, power_im = (
                    power_re * square_re - power_im * square_im,
                    power_re * square_im + power_im * square_re,
                )
            square_re, square_im = (
                square_re * square_re - square_im * square_im,
                2.0 * square_re * square_im,
            )
            left //= 2
        power_re, power_im = through * power_re, through * power_im
        end_re, end_im = re[g], im[g]
        carried_re, carried_im = zero, zero
        for _ in range(BLOCKS - 1):
            full_re = end_re + power_re * carried_re - power_im * carried_im
            full_im = end_im + power_re * carried_im + power_im * carried_re
            carried_re = jnp.where(first_row, 0.0, pltpu.roll(full_re, 1, 0))
            carried_im = jnp.where(first_row, 0.0, pltpu.roll(full_im, 1, 0))
        start_re.append(carried_re)
        start_im.append(carried_im)

    re, im = start_re, start_im
    for step in range(steps):
        advance(step, re, im)
        for g in range(groups):
            total_ref[g, rows(step), :] = amplitude[g] * re[g]
    for g in range(groups):
        out_ref[:, pl.ds(g * LANES, LANES)] = total_ref[g].astype(out_ref.dtype)


def modal_call(parts, keep, coefficients, name):
    length, modes = parts[0].shape
    spare = -modes % LANES
    if spare:
        parts = [jnp.pad(part, ((0, 0), (0, spare))) for part in parts]
        coefficients = jnp.pad(coefficients, ((0, 0), (0, spare)))
    width = modes + spare
    modal = pl.pallas_call(
        functools.partial(modal_kernel, len(parts)),
        out_shape=jax.ShapeDtypeStruct((length, width), jnp.bfloat16),
        scratch_shapes=[pltpu.VMEM((width // LANES, length, LANES), jnp.float32)],
        cost_estimate=pl.CostEstimate(
            flops=40 * length * width, transcendentals=0, bytes_accessed=8 * length * width
        ),
        compiler_params=pltpu.CompilerParams(vmem_limit_bytes=SMALL_GRANT),
        name=name,
    )(*parts, keep, coefficients)
    return modal[:, :modes] if spare else modal


def loads_kernel(last, matrix_ref, *refs):
    z, end = line_place()
    x = lax.axis_index("sub")
    rows = matrix_ref.shape[0] // 2
    if last:
        so_far_ref, across_ref, from_mid_ref, far_ref, from_end_ref, send_ref, stay_ref = refs
        shards = (
            (jnp.where(z < 2, 2, 1), jnp.where(end, from_mid_ref[...], across_ref[...])),
            (jnp.where(z < 2, 3, 0), jnp.where(end, from_end_ref[...], far_ref[...])),
        )
        outs = ((1 - x, send_ref), (x, stay_ref))
    else:
        own_ref, near_ref, out_ref = refs
        shards = ((z, own_ref[...]), (z + 1 - 2 * (z % 2), near_ref[...]))
        outs = ((1 - x, out_ref.at[0]), (x, out_ref.at[1]))
    for half, (part, out_ref) in enumerate(outs):
        first = pl.multiple_of(part * rows, 16)
        total = so_far_ref[half] if last else None
        for position, shard in shards:
            width = shard.shape[1]
            start = pl.multiple_of(position * width, LANES)
            product = lax.dot_general(
                shard,
                matrix_ref[pl.ds(first, rows), pl.ds(start, width)],
                (((1,), (1,)), ((), ())),
                preferred_element_type=jnp.float32,
            )
            total = product if total is None else total + product
        out_ref[...] = total.astype(out_ref.dtype)


def loads_call(last, matrix, operands, name):
    rows, modes = matrix.shape
    length = operands[-1].shape[0]
    half = (length, rows // 2)
    out_shape = (
        [jax.ShapeDtypeStruct(half, jnp.bfloat16), jax.ShapeDtypeStruct(half, jnp.float32)]
        if last
        else jax.ShapeDtypeStruct((2,) + half, jnp.float32)
    )
    return pl.pallas_call(
        functools.partial(loads_kernel, last),
        out_shape=out_shape,
        cost_estimate=pl.CostEstimate(
            flops=length * rows * modes, transcendentals=0, bytes_accessed=2 * rows * modes
        ),
        compiler_params=pltpu.CompilerParams(vmem_limit_bytes=GRANT),
        name=name,
    )(matrix, *operands)


def recurrence(frequency, damping, span_id):
    length = span_id.shape[1]
    decay_rate = frequency * damping
    magnitude = jnp.exp(-decay_rate)
    coefficients = jnp.stack(
        [
            magnitude * jnp.cos(frequency),
            magnitude * jnp.sin(frequency),
            jnp.sqrt(2.0 * decay_rate + 2.0 / length),
        ]
    )
    same = jnp.pad(span_id[:, 1:] == span_id[:, :-1], ((0, 0), (1, 0)))
    keep = jnp.broadcast_to(same.astype(jnp.float32)[:, :, None], span_id.shape + (LANES,))
    return coefficients, keep


def line_body(
    case_index, library, zone, gain, fluctuation, shapes, frequency, damping, span_id, matrix
):
    members = fluctuation.shape[0]
    own = shapes.shape[1] // 4
    z = lax.axis_index("panel")
    inner = [(0, 1), (1, 0), (2, 3), (3, 2)]
    inward = [(0, 1), (3, 2)]
    outward = [(1, 0), (2, 3)]
    middle = [(1, 2), (2, 1)]

    def move(value, pairs, name):
        with jax.named_scope(name):
            return lax.ppermute(value, "panel", pairs)

    coefficients, keep = recurrence(
        lax.dynamic_slice_in_dim(frequency, z * own, own, 0),
        lax.dynamic_slice_in_dim(damping, z * own, own, 0),
        span_id,
    )
    kinds = [jnp.bfloat16] * 3 + [jnp.float32]
    modal, element = [], []
    for m in range(members):
        out0, out1, out2, mine = forces_call(
            m, case_index, library, zone, gain, fluctuation, shapes, kinds
        )
        first = move(out0, inner, f"first{m}")
        second = move(out1, inward, f"second{m}")
        far = move(small_call(add_kernel, out1, first, f"addf{m}"), middle, f"far{m}")
        near = move(small_call(add_kernel, out2, second, f"addn{m}"), middle, f"near{m}")
        third = move(small_call(choose_kernel, out2, far, f"choose{m}"), inner, f"third{m}")
        own_modal = modal_call([mine, third, first, near], keep[m], coefficients, f"modal{m}")
        modal.append(own_modal)
        pair = move(own_modal, inner, f"pair{m}")
        across = move(own_modal, middle, f"across{m}")
        across_end = move(pair, middle, f"acrossend{m}")
        from_mid = move(across, outward, f"frommid{m}")
        from_end = move(across_end, outward, f"fromend{m}")
        so_far = loads_call(False, matrix, [own_modal, pair], f"loadsa{m}")
        send, stay = loads_call(
            True, matrix, [so_far, across, from_mid, across_end, from_end], f"loadsb{m}"
        )
        with jax.named_scope(f"rows{m}"):
            got = lax.ppermute(send, "sub", [(0, 1), (1, 0)])
        element.append((stay + got.astype(jnp.float32)).astype(jnp.bfloat16))
    return jnp.stack(modal)[:, :, None, :], jnp.stack(element)


def general_body(
    case_index, library, zone, gain, fluctuation, shapes, frequency, damping, span_id, matrix
):
    members, length, _ = fluctuation.shape
    own = shapes.shape[1] // lax.axis_size("panel")
    z = lax.axis_index("panel")
    coefficients, keep = recurrence(
        lax.dynamic_slice_in_dim(frequency, z * own, own, 0),
        lax.dynamic_slice_in_dim(damping, z * own, own, 0),
        span_id,
    )
    partial = jnp.concatenate(
        [
            forces_call(m, case_index, library, zone, gain, fluctuation, shapes, [jnp.float32])[0]
            for m in range(members)
        ],
        axis=0,
    )
    forces = jnp.transpose(
        lax.psum_scatter(jnp.transpose(partial), "panel", scatter_dimension=0, tiled=True)
    )
    modal = [
        modal_call([forces[m * length : (m + 1) * length]], keep[m], coefficients, f"modal{m}")
        for m in range(members)
    ]
    responses = jnp.stack(modal)[:, :, None, :]
    flat = jnp.transpose(jnp.concatenate(modal, axis=0))
    partial_loads = jnp.dot(
        matrix,
        lax.all_gather(flat, "panel", axis=0, tiled=True),
        preferred_element_type=jnp.float32,
    )
    sums = lax.psum_scatter(partial_loads, "sub", scatter_dimension=0, tiled=True)
    element = jnp.transpose(sums.astype(jnp.bfloat16)).reshape(members, length, -1)
    return responses, element


def solution(mesh):
    in_specs = (
        P(("runs", "case")),
        P(),
        P("panel"),
        P(("runs", "case"), "panel"),
        P(("runs", "case"), None, "panel"),
        P("panel", "sub"),
        P("sub"),
        P(("runs", "sub")),
        P(("runs", "case"), None),
        P("panel", "sub"),
    )
    out_specs = (
        P(("runs", "case"), None, "sub", "panel"),
        P(("runs", "case"), None, ("panel", "sub")),
    )
    line = mesh.shape["panel"] == 4 and mesh.shape["sub"] == 2
    return jax.shard_map(
        line_body if line else general_body,
        mesh=mesh,
        in_specs=in_specs,
        out_specs=out_specs,
        check_vma=False,
    )
```

```python
import functools

import jax
import jax.numpy as jnp
from jax import lax
from jax.experimental import pallas as pl
from jax.experimental.pallas import tpu as pltpu
from jax.sharding import PartitionSpec as P


BLOCKS = 8
LANES = 128
GRANT = 16 << 20
SMALL_GRANT = 4 << 20
SHARES, CUTS, LAST_PARTS = 32, (0, 14, 26, 32), 1


def line_place():
    z = lax.axis_index("panel")
    return z, (z == 0) | (z == 3)


def line_order(z):
    far = jnp.where(z < 2, 3, 0)
    inner = (z == 1) | (z == 2)
    return (
        jnp.where(z % 2 == 0, 3, 0),
        jnp.where(inner, far, jnp.where(z == 0, 2, 1)),
        jnp.where(z % 2 == 0, 1, 2),
        z,
    )


def forces_kernel(
    cuts, wanted, pieces, ends_only, index_ref, library_ref, zone_ref, gain_ref, fluctuation_ref, shapes_ref, *refs
):
    out_refs, scratch = refs[: len(wanted)], refs[len(wanted) :]
    index_at, library_at, zone_at, gain_at, fluctuation_at, pressure_at, columns_at, sems = scratch
    length = fluctuation_at.shape[1]
    cases = lambda slab: range(cuts[slab] // length, (cuts[slab + 1] - 1) // length + 1)
    width = columns_at.shape[2]
    order = line_order(line_place()[0]) if pieces > 1 else (0,)

    def run():
        moves = {
            "index": (index_ref, index_at),
            "zone": (zone_ref, zone_at),
            "gain": (gain_ref, gain_at),
            "library": (library_ref, library_at),
        }
        for slab, slot in wanted:
            for m in cases(slab):
                if ("fluctuation", m) not in moves:
                    moves["fluctuation", m] = (fluctuation_ref.at[m], fluctuation_at.at[m])
            if ("columns", slot) not in moves:
                start = order[slot] * width if pieces > 1 else 0
                moves["columns", slot] = (
                    shapes_ref.at[:, pl.ds(pl.multiple_of(start, LANES), width)],
                    columns_at.at[slot],
                )
        copies = {
            key: pltpu.make_async_copy(source, target, sems.at[i])
            for i, (key, (source, target)) in enumerate(moves.items())
        }
        for copy in copies.values():
            copy.start()
        arrived = set()

        def arrive(key):
            if key not in arrived:
                arrived.add(key)
                copies[key].wait()

        arrive("zone")
        zones, panels = library_at.shape[1], zone_at.shape[1]
        onehot = (
            lax.broadcasted_iota(jnp.int32, (zones, panels), 0) == zone_at[...]
        ).astype(jnp.bfloat16)
        ready = set()
        for (slab, slot), out_ref in zip(wanted, out_refs):
            for m in cases(slab):
                if m in ready:
                    continue
                ready.add(m)
                arrive("index")
                arrive("library")
                spread = lax.dot_general(
                    library_at[index_at[m]], onehot, (((0,), (0,)), ((), ())), preferred_element_type=jnp.float32
                )
                arrive("gain")
                arrive(("fluctuation", m))
                gain = gain_at[m : m + 1, :]
                pressure_at[m * length : (m + 1) * length, :] = (
                    gain * spread + fluctuation_at[m].astype(jnp.float32)
                ).astype(jnp.bfloat16)
            arrive(("columns", slot))
            out_ref[...] = jnp.dot(
                pressure_at[cuts[slab] : cuts[slab + 1], :],
                columns_at[slot],
                preferred_element_type=jnp.float32,
            ).astype(out_ref.dtype)

    if ends_only:
        pl.when(line_place()[1])(run)
    else:
        run()


def stay(value):
    return pltpu.with_memory_space_constraint(value, pltpu.HBM)


def forces_call(
    cuts, wanted, pieces, ends_only, case_index, library, zone, gain, fluctuation, shapes, kinds
):
    length = library.shape[2]
    members = fluctuation.shape[0]
    panels, modes = shapes.shape
    width = modes // pieces
    outs = pl.pallas_call(
        functools.partial(forces_kernel, cuts, wanted, pieces, ends_only),
        in_specs=[pl.BlockSpec(memory_space=pl.ANY)] * 6,
        out_shape=[
            jax.ShapeDtypeStruct((cuts[slab + 1] - cuts[slab], width), kinds[slot])
            for slab, slot in wanted
        ],
        scratch_shapes=[
            pltpu.SMEM((members,), jnp.int32),
            pltpu.VMEM(library.shape, library.dtype),
            pltpu.VMEM((1, panels), zone.dtype),
            pltpu.VMEM(gain.shape, gain.dtype),
            pltpu.VMEM((members, length, panels), fluctuation.dtype),
            pltpu.VMEM((members * length, panels), jnp.bfloat16),
            pltpu.VMEM((pieces, panels, width), shapes.dtype),
            pltpu.SemaphoreType.DMA((4 + members + pieces,)),
        ],
        cost_estimate=pl.CostEstimate(
            flops=2 * len(wanted) * length * panels * width,
            transcendentals=0,
            bytes_accessed=2 * (panels * modes + length * (modes + panels)),
        ),
        compiler_params=pltpu.CompilerParams(vmem_limit_bytes=GRANT),
    )(*[stay(value) for value in (case_index, library, zone[None, :], gain, fluctuation, shapes)])
    return dict(zip(wanted, outs))


def added(refs):
    total = refs[0][...].astype(jnp.float32)
    for ref in refs[1:]:
        total = total + ref[...].astype(jnp.float32)
    return total


def add_kernel(*refs):
    refs[-1][...] = added(refs[:-1]).astype(refs[-1].dtype)


def choose_kernel(end_ref, *refs):
    inner_refs, out_ref = refs[:-1], refs[-1]
    _, end = line_place()

    @pl.when(end)
    def _():
        out_ref[...] = end_ref[...]

    @pl.when(jnp.logical_not(end))
    def _():
        out_ref[...] = added(inner_refs).astype(out_ref.dtype)


def small_call(kernel, operands):
    first = operands[0]
    return pl.pallas_call(
        kernel,
        out_shape=jax.ShapeDtypeStruct(first.shape, first.dtype),
        cost_estimate=pl.CostEstimate(
            flops=first.size, transcendentals=0, bytes_accessed=6 * first.size
        ),
        compiler_params=pltpu.CompilerParams(vmem_limit_bytes=SMALL_GRANT),
    )(*operands)


def modal_kernel(offset, count, resumes, goes_on, *refs):
    part_refs, refs = refs[:count], refs[count:]
    state_ref = None
    if resumes:
        state_ref, refs = refs[0], refs[1:]
    keep_ref, coef_ref, out_ref, total_ref = refs[0], refs[1], refs[2], refs[-1]
    length, modes = out_ref.shape
    steps = length // BLOCKS
    groups = modes // LANES
    first_row = lax.broadcasted_iota(jnp.int32, (BLOCKS, LANES), 0) == 0

    def rows(step):
        return pl.ds(step, BLOCKS, stride=steps)

    decay_re, decay_im, amplitude = [], [], []
    for g in range(groups):
        at = pl.ds(g * LANES, LANES)
        total = part_refs[0][:, at]
        if count > 1:
            total = total + part_refs[1][:, at].astype(jnp.float32)
            near = part_refs[2][:, at].astype(jnp.float32)
            total = total + jnp.where(line_place()[1], 0.0, near)
        total_ref[g] = total
        decay_re.append(jnp.broadcast_to(coef_ref[0:1, at], (BLOCKS, LANES)))
        decay_im.append(jnp.broadcast_to(coef_ref[1:2, at], (BLOCKS, LANES)))
        amplitude.append(jnp.broadcast_to(coef_ref[2:3, at], (BLOCKS, LANES)))

    def advance(step, re, im):
        keep = keep_ref[pl.ds(offset + step, BLOCKS, stride=steps), :]
        for g in range(groups):
            a, b = decay_re[g], decay_im[g]
            force = total_ref[g, rows(step), :]
            held_re, held_im = keep * re[g], keep * im[g]
            re[g] = (a * held_re - b * held_im) + force
            im[g] = b * held_re + a * held_im
        return keep

    zero = jnp.zeros((BLOCKS, LANES), jnp.float32)
    re, im = [zero] * groups, [zero] * groups
    through = jnp.ones((BLOCKS, LANES), jnp.float32)
    for step in range(steps):
        through = through * advance(step, re, im)

    start_re, start_im = [], []
    for g in range(groups):
        power_re, power_im = jnp.ones_like(zero), zero
        square_re, square_im = decay_re[g], decay_im[g]
        left = steps
        while left:
            if left % 2:
                power_re, power_im = (
                    power_re * square_re - power_im * square_im,
                    power_re * square_im + power_im * square_re,
                )
            square_re, square_im = (
                square_re * square_re - square_im * square_im,
                2.0 * square_re * square_im,
            )
            left //= 2
        power_re, power_im = through * power_re, through * power_im
        end_re, end_im = re[g], im[g]
        entry_re, entry_im = 0.0, 0.0
        if resumes:
            at = pl.ds(g * LANES, LANES)
            entry_re = jnp.broadcast_to(state_ref[0:1, at], (BLOCKS, LANES))
            entry_im = jnp.broadcast_to(state_ref[1:2, at], (BLOCKS, LANES))
        carried_re = jnp.where(first_row, entry_re, zero)
        carried_im = jnp.where(first_row, entry_im, zero)
        for _ in range(BLOCKS - 1):
            full_re = end_re + power_re * carried_re - power_im * carried_im
            full_im = end_im + power_re * carried_im + power_im * carried_re
            carried_re = jnp.where(first_row, entry_re, pltpu.roll(full_re, 1, 0))
            carried_im = jnp.where(first_row, entry_im, pltpu.roll(full_im, 1, 0))
        start_re.append(carried_re)
        start_im.append(carried_im)

    re, im = start_re, start_im
    for step in range(steps):
        advance(step, re, im)
        for g in range(groups):
            total_ref[g, rows(step), :] = amplitude[g] * re[g]
    for g in range(groups):
        at = pl.ds(g * LANES, LANES)
        out_ref[:, at] = total_ref[g].astype(out_ref.dtype)
        if goes_on:
            refs[3][0:1, at] = re[g][BLOCKS - 1 :, :]
            refs[3][1:2, at] = im[g][BLOCKS - 1 :, :]


def modal_call(offset, parts, state, goes_on, keep, coefficients):
    length, modes = parts[0].shape
    spare = -modes % LANES
    if spare:
        parts = [jnp.pad(part, ((0, 0), (0, spare))) for part in parts]
    width = modes + spare
    resumes = state is not None
    out_shape = [
        jax.ShapeDtypeStruct((length, width), jnp.bfloat16),
        jax.ShapeDtypeStruct((2, width), jnp.float32),
    ]
    modal, *left = pl.pallas_call(
        functools.partial(modal_kernel, offset, len(parts), resumes, goes_on),
        out_shape=out_shape if goes_on else out_shape[:1],
        scratch_shapes=[pltpu.VMEM((width // LANES, length, LANES), jnp.float32)],
        cost_estimate=pl.CostEstimate(
            flops=40 * length * width, transcendentals=0, bytes_accessed=8 * length * width
        ),
        compiler_params=pltpu.CompilerParams(vmem_limit_bytes=SMALL_GRANT),
    )(*parts, *([state] if resumes else []), keep, coefficients)
    return (modal[:, :modes] if spare else modal), (left[0] if goes_on else None)


def split_kernel(value_ref, *out_refs):
    rows = out_refs[0].shape[0]
    for i, out_ref in enumerate(out_refs):
        out_ref[...] = value_ref[i * rows : (i + 1) * rows, :]


def split_call(value, parts):
    rows, width = value.shape
    return pl.pallas_call(
        split_kernel,
        out_shape=[jax.ShapeDtypeStruct((rows // parts, width), value.dtype)] * parts,
        cost_estimate=pl.CostEstimate(
            flops=value.size, transcendentals=0, bytes_accessed=4 * value.size
        ),
        compiler_params=pltpu.CompilerParams(vmem_limit_bytes=SMALL_GRANT),
    )(value)


def against(total, shard, matrix_ref, part, rows, position):
    width = shard.shape[1]
    first = pl.multiple_of(part * rows, 16)
    start = pl.multiple_of(position * width, LANES)
    product = lax.dot_general(
        shard,
        matrix_ref[pl.ds(first, rows), pl.ds(start, width)],
        (((1,), (1,)), ((), ())),
        preferred_element_type=jnp.float32,
    )
    return product if total is None else total + product


def loads_kernel(matrix_ref, own_ref, near_ref, out_ref):
    z, _ = line_place()
    x = lax.axis_index("sub")
    rows = matrix_ref.shape[0] // 2
    for half, part in enumerate((1 - x, x)):
        total = against(None, own_ref[...], matrix_ref, part, rows, z)
        out_ref[half] = against(total, near_ref[...], matrix_ref, part, rows, z + 1 - 2 * (z % 2))


def last_loads_kernel(
    offset, matrix_ref, so_far_ref, across_ref, from_mid_ref, far_ref, from_end_ref, send_ref, keep_ref
):
    z, end = line_place()
    x = lax.axis_index("sub")
    rows = matrix_ref.shape[0] // 2
    length = send_ref.shape[0]
    at = slice(offset * length, (offset + 1) * length)
    middle = jnp.where(end, from_mid_ref[at, :], across_ref[at, :])
    far = jnp.where(end, from_end_ref[...], far_ref[...])
    for half, (part, out_ref) in enumerate(((1 - x, send_ref), (x, keep_ref))):
        total = against(
            so_far_ref[half, at, :], middle, matrix_ref, part, rows, jnp.where(z < 2, 2, 1)
        )
        total = against(total, far, matrix_ref, part, rows, jnp.where(z < 2, 3, 0))
        out_ref[...] = total.astype(out_ref.dtype)


def loads_call(matrix, operands):
    rows, modes = matrix.shape
    length = operands[0].shape[0]
    return pl.pallas_call(
        loads_kernel,
        out_shape=jax.ShapeDtypeStruct((2, length, rows // 2), jnp.float32),
        cost_estimate=pl.CostEstimate(
            flops=length * rows * modes, transcendentals=0, bytes_accessed=2 * rows * modes
        ),
        compiler_params=pltpu.CompilerParams(vmem_limit_bytes=GRANT),
    )(matrix, *operands)


def last_loads_call(matrix, operands, offset):
    rows, modes = matrix.shape
    length = operands[-1].shape[0]
    half = (length, rows // 2)
    return pl.pallas_call(
        functools.partial(last_loads_kernel, offset),
        out_shape=[
            jax.ShapeDtypeStruct(half, jnp.bfloat16),
            jax.ShapeDtypeStruct(half, jnp.float32),
        ],
        cost_estimate=pl.CostEstimate(
            flops=length * rows * modes, transcendentals=0, bytes_accessed=2 * rows * modes
        ),
        compiler_params=pltpu.CompilerParams(vmem_limit_bytes=GRANT),
    )(matrix, *operands)


def prepare_kernel(frequency_ref, damping_ref, span_ref, coef_ref, keep_ref):
    own = coef_ref.shape[1]
    if frequency_ref.shape[1] == own:
        at = slice(None)
    else:
        at = pl.ds(pl.multiple_of(lax.axis_index("panel") * own, LANES), own)
    frequency, damping = frequency_ref[:, at], damping_ref[:, at]
    members, length = span_ref.shape
    decay_rate = frequency * damping
    magnitude = jnp.exp(-decay_rate)
    coef_ref[0:1, :] = magnitude * jnp.cos(frequency)
    coef_ref[1:2, :] = magnitude * jnp.sin(frequency)
    coef_ref[2:3, :] = jnp.sqrt(2.0 * decay_rate + 2.0 / length)
    for m in range(members):
        span = span_ref[m : m + 1, :]
        same = (span == pltpu.roll(span, 1, 1)) & (
            lax.broadcasted_iota(jnp.int32, span.shape, 1) > 0
        )
        row = jnp.where(same, 1.0, 0.0)
        keep_ref[m * length : (m + 1) * length, :] = jnp.transpose(jnp.broadcast_to(row, (LANES, length)))


def prepare_call(frequency, damping, span_id, own):
    members, length = span_id.shape
    return pl.pallas_call(
        prepare_kernel,
        out_shape=[
            jax.ShapeDtypeStruct((3, own), jnp.float32),
            jax.ShapeDtypeStruct((members * length, LANES), jnp.float32),
        ],
        cost_estimate=pl.CostEstimate(
            flops=100 * own, transcendentals=4 * own, bytes_accessed=4 * members * length * LANES
        ),
        compiler_params=pltpu.CompilerParams(vmem_limit_bytes=SMALL_GRANT),
        name="prepare",
    )(frequency[None, :], damping[None, :], span_id)


def line_body(*args):
    return line_steps(*args)


def line_steps(
    case_index, library, zone, gain, fluctuation, shapes, frequency, damping, span_id, matrix
):
    members = fluctuation.shape[0]
    own = shapes.shape[1] // 4
    inner = [(0, 1), (1, 0), (2, 3), (3, 2)]
    inward = [(0, 1), (3, 2)]
    outward = [(1, 0), (2, 3)]
    skip = [(0, 2), (3, 1)]
    cores = lax.axis_size("case")
    at = lambda place, core: place * cores + core
    middle = [(at(a, c), at(3 - a, c)) for a in (1, 2) for c in range(cores)]
    middle += [(at(a, c), at(a, (c + 1) % cores)) for a in (0, 3) for c in range(cores)]

    def move(value, pairs):
        return lax.ppermute(value, ("panel", "case") if pairs is middle else "panel", pairs)

    coefficients, keep = prepare_call(frequency, damping, span_id, own)
    kinds = [jnp.bfloat16] * 3 + [jnp.float32]
    arguments = (case_index, library, zone, gain, fluctuation, shapes, kinds)
    steps = members * fluctuation.shape[1]
    cuts = tuple(steps * share // SHARES for share in CUTS)
    slabs = len(cuts) - 1
    early = ((0, 0),)
    late = tuple((k, slot) for k in range(slabs) for slot in (1, 0, 2, 3))
    head = forces_call(cuts, early, 4, True, *arguments)
    pieces = forces_call(cuts, late, 4, False, *arguments)
    modal, element, state = [], [], None
    for m in range(slabs):
        part = [pieces[m, slot] for slot in range(4)]
        if m == 0:
            direct = move(head[m, 0], skip)
            far = move(part[1], middle)
            outer = [part[0], direct, far]
        else:
            first = move(part[0], inward)
            far = move(small_call(add_kernel, [part[1], first]), middle)
            outer = [part[0], far]
        second = move(part[1], inward)
        near = move(small_call(add_kernel, [part[2], second]), middle)
        third = move(small_call(choose_kernel, [part[2], *outer]), inner)
        own_modal, state = modal_call(
            cuts[m], [part[3], third, near], state, m < slabs - 1, keep, coefficients
        )
        modal.append(own_modal)
        pair = move(own_modal, inner)
        across = move(own_modal, middle)
        across_end = move(pair, middle)
        from_mid = move(across, outward)
        so_far = loads_call(matrix, [own_modal, pair])
        halves = 1 if m < slabs - 1 else LAST_PARTS
        tails = [across_end] if halves == 1 else split_call(across_end, halves)
        for half, tail in enumerate(tails):
            far_end = move(tail, outward)
            send, keeps = last_loads_call(matrix, [so_far, across, from_mid, tail, far_end], half)
            got = lax.ppermute(send, "sub", [(0, 1), (1, 0)])
            element.append((keeps + got.astype(jnp.float32)).astype(jnp.bfloat16))
    element = jnp.concatenate(element, axis=0)
    shape = fluctuation.shape[:2]
    return jnp.concatenate(modal, axis=0).reshape(shape + (1, -1)), element.reshape(shape + (-1,))


def general_body(
    case_index, library, zone, gain, fluctuation, shapes, frequency, damping, span_id, matrix
):
    members, length, _ = fluctuation.shape
    own = shapes.shape[1] // lax.axis_size("panel")
    z = lax.axis_index("panel")
    spare = -own % LANES
    local = lambda value: jnp.pad(lax.dynamic_slice_in_dim(value, z * own, own, 0), (0, spare))
    coefficients, keep = prepare_call(local(frequency), local(damping), span_id, own + spare)
    wanted = tuple((m, 0) for m in range(members))
    cuts = tuple(m * length for m in range(members + 1))
    pieces = forces_call(
        cuts, wanted, 1, False, case_index, library, zone, gain, fluctuation, shapes, [jnp.float32]
    )
    partial = jnp.concatenate([pieces[key] for key in wanted], axis=0)
    forces = jnp.transpose(
        lax.psum_scatter(jnp.transpose(partial), "panel", scatter_dimension=0, tiled=True)
    )
    modal = [
        modal_call(
            m * length, [forces[m * length : (m + 1) * length]], None, False, keep, coefficients
        )[0]
        for m in range(members)
    ]
    responses = jnp.stack(modal)[:, :, None, :]
    flat = jnp.transpose(jnp.concatenate(modal, axis=0))
    partial_loads = jnp.dot(
        matrix,
        lax.all_gather(flat, "panel", axis=0, tiled=True),
        preferred_element_type=jnp.float32,
    )
    sums = lax.psum_scatter(partial_loads, "sub", scatter_dimension=0, tiled=True)
    element = jnp.transpose(sums.astype(jnp.bfloat16)).reshape(members, length, -1)
    return responses, element


def solution(mesh):
    in_specs = (
        P(("runs", "case")),
        P(),
        P("panel"),
        P(("runs", "case"), "panel"),
        P(("runs", "case"), None, "panel"),
        P("panel", "sub"),
        P("sub"),
        P(("runs", "sub")),
        P(("runs", "case"), None),
        P("panel", "sub"),
    )
    out_specs = (
        P(("runs", "case"), None, "sub", "panel"),
        P(("runs", "case"), None, ("panel", "sub")),
    )
    line = mesh.shape["panel"] == 4 and mesh.shape["sub"] == 2
    return jax.shard_map(
        line_body if line else general_body,
        mesh=mesh,
        in_specs=in_specs,
        out_specs=out_specs,
        check_vma=False,
    )
```
